32 devices in a mesh: gx: 4 (over x, core), gy: 8 (over z, y).
Axes of the slice: x: 2, y: 2, z: 4, core: 2. Of those that a mesh axis runs over, the one named last changes fastest.
Arguments:
- right_side: bfloat16 [4, 8, 8, 625, 256], P('gx', 'gy'), may hold values from -6 to 6
- inverse_blocks: bfloat16 [4, 8, 8, 625, 625], P('gx', 'gy'), may hold values from -0.2 to 0.8
- lift_matrix: bfloat16 [625, 375], replicated, may hold values from -2 to 2
- plane_order: int32 [4, 8, 8], P('gx', 'gy'), may hold values from 0 to 7, each once within a row
- face_orient: int32 [4, 8, 8, 3], P('gx', 'gy'), may hold values from 0 to 7
Outputs:
- solution: bfloat16 [4, 8, 8, 625, 256], P('gx', 'gy')
The draws below stay inside these ranges and needn't reach their ends.
Inputs may be any that keep to these rules, and one draw needn't show every extreme that they name: `plane_order`: each slab's row lists the storage slots of its 8 elements from lowest to highest z, each slot once. `face_orient`: any of the eight orientations of a square face.
All inputs are finite; a program needn't handle non-finite values.
Results may differ from the reference program's by a relative error of at most 0.025.
Values may be sent and summed in bfloat16 or wider, within the bound.
A program may use at most 64 MiB of HBM per device.

```python
import jax
import jax.numpy as jnp
import numpy as np
from jax import lax

VARS = 5
NODES = 5
BLOCK = 625
FACE = 125
PLANES = 8
COLS = 256
SLABS_X = 4
SLABS_Y = 8


def draw_inverse_blocks(key, part):
    full_shape = (SLABS_X, SLABS_Y, PLANES, BLOCK, BLOCK)
    diag_key, rest_key = jax.random.split(jax.random.fold_in(key, 17))
    diagonal = jnp.exp(jax.random.uniform(diag_key, full_shape[:-1], jnp.float32, jnp.log(0.4), jnp.log(0.62)))
    coupling = jnp.clip(jax.random.normal(rest_key, full_shape, jnp.float32), -6.0, 6.0)
    identity = jnp.eye(BLOCK, dtype=jnp.float32)
    return (diagonal[..., None] * identity + 0.2 * coupling / jnp.sqrt(BLOCK * 1.0)).astype(jnp.bfloat16)


def draw_lift_matrix(key, part):
    lift_key = jax.random.fold_in(key, 29)
    full_shape = (BLOCK, 3 * FACE)
    entries = jnp.clip(jax.random.normal(lift_key, full_shape, jnp.float32), -6.0, 6.0)
    velocity = jnp.repeat(jnp.array([0.91, 1.29, 0.82], jnp.float32), FACE)
    return (entries * velocity[None, :] / jnp.sqrt(FACE * 1.0)).astype(jnp.bfloat16)


def set_ends(drawn, rng, least, high):
    extent = drawn.shape
    index_at = [jax.random.randint(jax.random.fold_in(rng, axis), (), 0, extent[axis]) for axis in range(len(extent))]
    drawn = drawn.at[tuple(index_at)].set(least)
    longest = extent.index(max(extent))
    index_at[longest] = (index_at[longest] + 1) % extent[longest]
    return drawn.at[tuple(index_at)].set(high)


def block_scale(own_key, dims, shards, smallest, top_value):
    loudness = 1.0
    for position, parts in shards:
        draws = jax.random.uniform(jax.random.fold_in(jax.random.fold_in(own_key, 6), position), (parts,), jnp.float32, smallest / len(shards), top_value / len(shards))
        loudness = loudness * jnp.repeat(jnp.exp(draws), dims[position] // parts).reshape((-1,) + (1,) * (len(dims) - 1 - position))
    return loudness


def noise(stream_key, dims, scale, limit, pieces=(), kind=jnp.bfloat16):
    values = jax.random.normal(stream_key, dims, jnp.float32) * scale
    if len(pieces) > 0:
        values = block_scale(stream_key, dims, pieces, -0.22, 0.18) * values
    return jnp.clip(values, min=-limit, max=limit).astype(kind)


def setup_inputs(seed: int = 0) -> dict:
    streams_of = jax.random.split(jax.random.key(seed), 6)
    right_side = noise(streams_of[0], (SLABS_X, SLABS_Y, PLANES, BLOCK, COLS), 1.0, 6.0, ((0, 4), (1, 8)))
    inverse_blocks = draw_inverse_blocks(jax.random.fold_in(streams_of[5], 71), 0)
    lift_matrix = draw_lift_matrix(jax.random.fold_in(streams_of[5], 71), 0)
    plane_order = jax.vmap(lambda own: jax.random.permutation(own, PLANES))(jax.random.split(streams_of[3], SLABS_X * SLABS_Y)).reshape((SLABS_X, SLABS_Y, PLANES)).astype(jnp.int32)
    face_orient = set_ends(jax.random.randint(streams_of[4], (SLABS_X, SLABS_Y, PLANES, 3), 0, 8), jax.random.fold_in(streams_of[4], 1), 0, 7).astype(jnp.int32)
    return dict(right_side=right_side, inverse_blocks=inverse_blocks, lift_matrix=lift_matrix, plane_order=plane_order, face_orient=face_orient)


def orient_table():
    lookup_table = np.zeros((8, FACE), np.int32)
    for orient in range(8):
        for variable in range(VARS):
            for first in range(NODES):
                for second in range(NODES):
                    if orient & 1:
                        first_new, second_new = second, first
                    else:
                        first_new, second_new = first, second
                    if orient & 2:
                        first_new = NODES - 1 - first_new
                    if orient & 4:
                        second_new = NODES - 1 - second_new
                    target = variable * NODES * NODES + first * NODES + second
                    lookup_table[orient, target] = variable * NODES * NODES + first_new * NODES + second_new
    return lookup_table


def select_matrices(orients):
    lookup = jnp.asarray(orient_table())
    codes = jnp.arange(8, dtype=jnp.int32)[:, None]
    chosen = jnp.sum(jnp.where(orients[..., None, None] == codes, lookup, 0), axis=-2)
    return (chosen[..., None] == jnp.arange(FACE, dtype=jnp.int32)).astype(jnp.float32)


def face_traces(block):
    leading = block.shape[:-2]
    columns = block.shape[-1]
    shaped = block.reshape(leading + (VARS, NODES, NODES, NODES, columns))
    along_x = shaped[..., :, NODES - 1, :, :, :].reshape(leading + (FACE, columns))
    along_y = shaped[..., :, :, NODES - 1, :, :].reshape(leading + (FACE, columns))
    along_z = shaped[..., :, :, :, NODES - 1, :].reshape(leading + (FACE, columns))
    return jnp.stack([along_x, along_y, along_z], axis=-3)


def reference(right_side, inverse_blocks, lift_matrix, plane_order, face_orient):
    across = jnp.arange(SLABS_X, dtype=jnp.int32)
    solution = jnp.zeros(right_side.shape, jnp.bfloat16)
    z_traces = jnp.zeros((SLABS_X, SLABS_Y, FACE, COLS), jnp.bfloat16)
    lift_wide = lift_matrix.astype(jnp.float32)
    for plane in range(PLANES):
        slots = plane_order[:, :, plane]
        z_before = z_traces

        def diagonal(carry, sweep):
            x_traces, y_traces, next_z, solution = carry
            column = sweep - across
            is_live = (column >= 0) & (column < SLABS_Y)
            clipped = jnp.clip(column, 0, SLABS_Y - 1).astype(jnp.int32)
            left_slab = jnp.maximum(across - 1, 0).astype(jnp.int32)
            below_slab = jnp.maximum(clipped - 1, 0).astype(jnp.int32)
            from_x = jnp.where((across > 0)[:, None, None], x_traces[left_slab, clipped], 0)
            from_y = jnp.where((clipped > 0)[:, None, None], y_traces[across, below_slab], 0)
            from_z = z_before[across, clipped]
            slot_ids = slots[across, clipped]
            source_rows = right_side[across, clipped, slot_ids]
            blocks = inverse_blocks[across, clipped, slot_ids]
            orients = face_orient[across, clipped, slot_ids]
            incoming = jnp.stack([from_x, from_y, from_z], axis=1).astype(jnp.float32)
            select = select_matrices(orients)
            turned = jnp.einsum('edqc,edcn->edqn', select, incoming).astype(jnp.bfloat16)
            turned = turned.reshape(SLABS_X, 3 * FACE, COLS).astype(jnp.float32)
            source = (source_rows.astype(jnp.float32) - jnp.einsum('bq,eqn->ebn', lift_wide, turned)).astype(jnp.bfloat16)
            result = jnp.einsum('ebc,ecn->ebn', blocks.astype(jnp.float32), source.astype(jnp.float32)).astype(jnp.bfloat16)
            traces = face_traces(result)
            live_mask = is_live[:, None, None]
            x_traces = x_traces.at[across, clipped].set(jnp.where(live_mask, traces[:, 0], x_traces[across, clipped]))
            y_traces = y_traces.at[across, clipped].set(jnp.where(live_mask, traces[:, 1], y_traces[across, clipped]))
            next_z = next_z.at[across, clipped].set(jnp.where(live_mask, traces[:, 2], next_z[across, clipped]))
            solution = solution.at[across, clipped, slot_ids].set(jnp.where(live_mask, result, solution[across, clipped, slot_ids]))
            return (x_traces, y_traces, next_z, solution), None

        blank = jnp.zeros((SLABS_X, SLABS_Y, FACE, COLS), jnp.bfloat16)
        finished, unused = lax.scan(diagonal, (blank, blank, blank, solution), jnp.arange(SLABS_X + SLABS_Y - 1, dtype=jnp.int32))
        z_traces = finished[2]
        solution = finished[3]
    return solution
```

```python
import functools

import jax
import jax.numpy as jnp
import numpy as np
from jax import lax
from jax.experimental import pallas as pl
from jax.experimental.pallas import tpu as pltpu
from jax.sharding import PartitionSpec as P

VARS = 5
NODES = 5
SQUARE = NODES * NODES
FACE = VARS * SQUARE
BLOCK = FACE * NODES
LANE = 128
MESH = pl.DeviceIdType.MESH


def orient_table():
    table = np.zeros((8, LANE, LANE), np.float32)
    for orient in range(8):
        for variable in range(VARS):
            for first in range(NODES):
                for second in range(NODES):
                    p, q = (second, first) if orient & 1 else (first, second)
                    if orient & 2:
                        p = NODES - 1 - p
                    if orient & 4:
                        q = NODES - 1 - q
                    target = variable * SQUARE + first * NODES + second
                    table[orient, target, variable * SQUARE + p * NODES + q] = 1.0
    return table


def dot(a, b):
    return jnp.dot(a, b, preferred_element_type=jnp.float32)


def row_chunks(block):
    return [(start, min(LANE, block - start)) for start in range(0, block, LANE)]


def sweep_kernel(
    order, orient, table_hbm, lift_hbm, rhs_hbm, inv_hbm, sol,
    table, lift, raw_r, raw_b, stage, rhs, inv, padded, turned, plain, wide, weight, part, trace_m, trace_r,
    inc, out, load_sem, r_sem, b_sem, x_send, y_send, x_recv, y_recv,
):
    planes, block, columns = rhs.shape
    parts = columns // LANE
    two, three = 2 * LANE, 3 * LANE
    chunks = row_chunks(block)
    tiles = [(t, min(LANE, block - t)) for t in range(0, block, LANE)]
    count_x, count_y = lax.axis_size("gx"), lax.axis_size("gy")
    me_x, me_y = lax.axis_index("gx"), lax.axis_index("gy")
    has_left, has_right = me_x > 0, me_x < count_x - 1
    has_below, has_above = me_y > 0, me_y < count_y - 1

    loads = [
        pltpu.make_async_copy(source, target, load_sem.at[i])
        for i, (source, target) in enumerate([(lift_hbm, lift), (table_hbm, table)])
    ]
    loads[0].start()

    def fetch(i, start, size):
        rows = pl.ds(start, size)
        return (
            pltpu.make_async_copy(rhs_hbm.at[rows], raw_r.at[rows], r_sem.at[i]),
            pltpu.make_async_copy(inv_hbm.at[rows], raw_b.at[rows], b_sem.at[i]),
        )

    for i, (start, size) in enumerate(chunks):
        for copy in fetch(i, start, size):
            copy.start()
    loads[1].start()

    barrier = pltpu.get_barrier_semaphore()
    for present, x, y in (
        (has_left, me_x - 1, me_y),
        (has_right, me_x + 1, me_y),
        (has_below, me_x, me_y - 1),
        (has_above, me_x, me_y + 1),
    ):
        @pl.when(present)
        def _():
            pl.semaphore_signal(barrier, inc=1, device_id=(x, y), device_id_type=MESH)

    part[...] = jnp.zeros_like(part)
    out[0] = jnp.zeros(out.shape[1:], out.dtype)
    for d in range(3):
        tail = (d + 1) * LANE - 8
        trace_r[:, :, tail : tail + 8, :] = jnp.zeros((planes, parts, 8, LANE), trace_r.dtype)

    @pl.when(me_x == 0)
    def _():
        inc[:, :, :LANE, :] = jnp.zeros((planes, parts, LANE, LANE), inc.dtype)

    @pl.when(me_y == 0)
    def _():
        inc[:, :, LANE:, :] = jnp.zeros((planes, parts, LANE, LANE), inc.dtype)

    row = lax.broadcasted_iota(jnp.int32, (3 * FACE, three), 0)
    col = lax.broadcasted_iota(jnp.int32, (3 * FACE, three), 1)
    face = jnp.where(col >= two, 2, jnp.where(col >= LANE, 1, 0))
    inside = col - face * LANE
    spread = ((inside < FACE) & (row == face * FACE + inside)).astype(jnp.float32).astype(jnp.bfloat16)
    loads[0].wait()
    padded[...] = lax.dot_general(
        lift[...], spread, (((0,), (0,)), ((), ())), preferred_element_type=jnp.float32
    ).astype(jnp.bfloat16)

    whole = block // LANE

    def split(raw, into, rows, size, lanes, t):
        mixed = raw[rows, :, lanes].astype(jnp.float32)
        wide_lanes = mixed.shape[-1]
        stage[t, : size * planes, :wide_lanes] = mixed.reshape(size * planes, wide_lanes)
        for s in range(planes):
            apart = stage[t, pl.ds(s, size, stride=planes), :]
            into[s, rows, lanes] = apart[:, :wide_lanes].astype(jnp.bfloat16)

    def arrange(i, start, size):
        for copy in fetch(i, start, size):
            copy.wait()
        rows = pl.ds(start, size)
        for t, (first, wide_lanes) in enumerate(tiles):
            split(raw_b, inv, rows, size, slice(first, first + wide_lanes), t)
        for t in range(columns // LANE):
            split(raw_r, rhs, rows, size, slice(t * LANE, (t + 1) * LANE), len(tiles) + t)

    def arrange_full(i, carry):
        arrange(i, pl.multiple_of(i * LANE, LANE), LANE)
        return carry

    lax.fori_loop(0, whole, arrange_full, 0)
    for i, (start, size) in list(enumerate(chunks))[whole:]:
        arrange(i, start, size)
    loads[1].wait()

    def pick(source, put):
        for v in range(VARS):
            put(v * SQUARE, source[pl.ds(v * FACE + FACE - SQUARE, SQUARE), :])
        for v in range(VARS * NODES):
            put(LANE + v * NODES, source[pl.ds(v * SQUARE + SQUARE - NODES, NODES), :])
        put(two, source[pl.ds(NODES - 1, FACE, stride=NODES), :])

    def prepare(k):
        slot = order[k]
        solved = dot(inv[slot], rhs[slot])
        for c in range(parts):
            plain[k, c] = solved[:, c * LANE : (c + 1) * LANE]

            def put_plain(start, rows):
                trace_r[k, c, pl.ds(start, rows.shape[0]), :] = rows

            pick(plain.at[k, c], put_plain)
        spreads = dot(inv[slot], padded[...])
        weight[k] = spreads.astype(jnp.bfloat16)
        for d in range(3):
            wide[d] = spreads[:, d * LANE : (d + 1) * LANE]

            def put_part(start, rows):
                part[d, pl.ds(start, rows.shape[0]), :] = rows

            pick(wide.at[d], put_part)
            moved = dot(part[d].astype(jnp.bfloat16), table[orient[d, 0, slot]])
            trace_m[k, :, d * LANE : (d + 1) * LANE] = moved.astype(jnp.bfloat16)

    def hop(k, c, axis):
        rows = pl.ds(axis * LANE, LANE)
        send, recv = ((x_send, x_recv), (y_send, y_recv))[axis]
        return pltpu.make_async_remote_copy(
            src_ref=out.at[k + 1, c, rows, :],
            dst_ref=inc.at[k, c, rows, :],
            send_sem=send.at[k, c],
            recv_sem=recv.at[k, c],
            device_id=((me_x + 1, me_y), (me_x, me_y + 1))[axis],
            device_id_type=MESH,
        )

    def advance(k, c):
        started = trace_r[k, c] - dot(trace_m[k, :, two:], out[k, c, two:, :])

        @pl.when(has_left)
        def _():
            hop(k, c, 0).wait_recv()

        @pl.when(has_below)
        def _():
            hop(k, c, 1).wait_recv()

        arrived = inc[k, c]
        ahead_rows = (started[:two] - dot(trace_m[k, :two, :two], arrived)).astype(jnp.bfloat16)
        out[k + 1, c, LANE:two, :] = ahead_rows[LANE:]

        @pl.when(has_above)
        def _():
            hop(k, c, 1).start()

        out[k + 1, c, :LANE, :] = ahead_rows[:LANE]

        @pl.when(has_right)
        def _():
            hop(k, c, 0).start()

        out[k + 1, c, two:, :] = (started[two:] - dot(trace_m[k, two:, :two], arrived)).astype(jnp.bfloat16)

    def finish(k):
        slot = order[k]
        faces = [[inc[k, c, d * LANE : (d + 1) * LANE, :] for c in range(parts)] for d in range(2)]
        faces.append([out[k, c, two:, :] for c in range(parts)])
        for d in range(3):
            face = jnp.concatenate(faces[d], axis=-1)
            turned[d * LANE : (d + 1) * LANE, :] = dot(table[orient[d, 0, slot]], face).astype(jnp.bfloat16)
        lifted = dot(weight[k], turned[...])
        for c in range(parts):
            sol[c, pl.ds(k, block, stride=planes), :] = plain[k, c] - lifted[:, c * LANE : (c + 1) * LANE]

    distance = me_x + me_y
    lead = jnp.minimum(1 + 2 * distance, planes)
    near = distance * 2 <= count_x + count_y - 2

    def ahead(k, carry):
        prepare(k)
        return carry

    lax.fori_loop(0, lead, ahead, 0)

    neighbours = sum(p.astype(jnp.int32) for p in (has_left, has_right, has_below, has_above))
    pl.semaphore_wait(barrier, neighbours)

    def step(k, carry):
        for c in range(parts):
            advance(k, c)

        @pl.when(k + lead < planes)
        def _():
            prepare(k + lead)

        @pl.when(jnp.logical_not(near))
        def _():
            finish(k)

        return carry

    lax.fori_loop(0, planes, step, 0)

    @pl.when(near)
    def _():
        def late(k, carry):
            finish(k)
            return carry

        lax.fori_loop(0, planes, late, 0)

    def drain(k, carry):
        for c in range(parts):
            @pl.when(has_right)
            def _():
                hop(k, c, 0).wait_send()

            @pl.when(has_above)
            def _():
                hop(k, c, 1).wait_send()
        return carry

    lax.fori_loop(0, planes, drain, 0)


def place_kernel(order, sol, out, ready, sems):
    block, planes, columns = ready.shape
    chunks = row_chunks(block)
    whole = block // LANE
    place_of = lax.broadcasted_iota(jnp.int32, (planes, LANE), 0)
    source = jnp.zeros((planes, LANE), jnp.int32)
    for k in range(planes):
        source = jnp.where(place_of == order[k], k, source)

    def put(i, start, size):
        rows = pl.ds(start, size)
        return pltpu.make_async_copy(ready.at[rows], out.at[rows], sems.at[i])

    def place(i, start, size):
        rows = pl.ds(start, size)
        picks = jnp.broadcast_to(source[None], (size, planes, LANE))
        for t in range(columns // LANE):
            lanes = slice(t * LANE, (t + 1) * LANE)
            swept = sol[t, pl.ds(start * planes, size * planes), :].reshape(size, planes, LANE)
            placed = jnp.take_along_axis(swept, picks, axis=1, mode="promise_in_bounds")
            ready[rows, :, lanes] = placed.astype(jnp.bfloat16)
        put(i, start, size).start()

    def place_full(i, carry):
        place(i, pl.multiple_of(i * LANE, LANE), LANE)
        return carry

    lax.fori_loop(0, whole, place_full, 0)
    for i, (start, size) in list(enumerate(chunks))[whole:]:
        place(i, start, size)
    for i, (start, size) in enumerate(chunks):
        put(i, start, size).wait()


def on_device(right_side, inverse_blocks, lift_matrix, plane_order, face_orient):
    rhs = jnp.transpose(right_side, (0, 1, 3, 2, 4))[0, 0]
    inv = jnp.transpose(inverse_blocks, (0, 1, 3, 2, 4))[0, 0]
    order = plane_order[0, 0]
    orient = jnp.transpose(face_orient, (0, 3, 1, 2))[0]
    block, planes, columns = rhs.shape
    tiles = pl.cdiv(block, LANE)
    chunks = len(row_chunks(block))
    parts = columns // LANE
    two, three = 2 * LANE, 3 * LANE
    bf16, f32 = jnp.bfloat16, jnp.float32
    table = jnp.asarray(orient_table(), bf16)
    lift = lift_matrix.T
    smem = pl.BlockSpec(memory_space=pltpu.SMEM)
    vmem = pl.BlockSpec(memory_space=pltpu.VMEM)
    anywhere = pl.BlockSpec(memory_space=pl.ANY)
    sol = pl.pallas_call(
        sweep_kernel,
        out_shape=pltpu.VMEM((parts, block * planes, LANE), f32),
        in_specs=[smem, smem] + [anywhere] * 4,
        out_specs=vmem,
        scratch_shapes=[
            pltpu.VMEM(table.shape, bf16),
            pltpu.VMEM(lift.shape, bf16),
            pltpu.VMEM(rhs.shape, bf16),
            pltpu.VMEM(inv.shape, bf16),
            pltpu.VMEM((tiles + columns // LANE, LANE * planes, LANE), f32),
            pltpu.VMEM((planes, block, columns), bf16),
            pltpu.VMEM((planes, block, block), bf16),
            pltpu.VMEM((block, three), bf16),
            pltpu.VMEM((three, columns), bf16),
            pltpu.VMEM((planes, parts, block, LANE), f32),
            pltpu.VMEM((3, block, LANE), f32),
            pltpu.VMEM((planes, block, three), bf16),
            pltpu.VMEM((3, three, LANE), f32),
            pltpu.VMEM((planes, three, three), bf16),
            pltpu.VMEM((planes, parts, three, LANE), f32),
            pltpu.VMEM((planes, parts, two, LANE), bf16),
            pltpu.VMEM((planes + 1, parts, three, LANE), bf16),
            pltpu.SemaphoreType.DMA((2,)),
            pltpu.SemaphoreType.DMA((chunks,)),
            pltpu.SemaphoreType.DMA((chunks,)),
            pltpu.SemaphoreType.DMA((planes, parts)),
            pltpu.SemaphoreType.DMA((planes, parts)),
            pltpu.SemaphoreType.DMA((planes, parts)),
            pltpu.SemaphoreType.DMA((planes, parts)),
        ],
        compiler_params=pltpu.CompilerParams(
            collective_id=0, has_side_effects=True, vmem_limit_bytes=54 * 1024 * 1024
        ),
    )(order, orient, table, lift, rhs, inv)
    result = pl.pallas_call(
        place_kernel,
        out_shape=jax.ShapeDtypeStruct(rhs.shape, bf16),
        in_specs=[smem, vmem],
        out_specs=anywhere,
        scratch_shapes=[
            pltpu.VMEM(rhs.shape, bf16),
            pltpu.SemaphoreType.DMA((chunks,)),
        ],
        compiler_params=pltpu.CompilerParams(vmem_limit_bytes=16 * 1024 * 1024),
    )(order, sol)
    return jnp.transpose(result[None, None], (0, 1, 3, 2, 4))


def solution(mesh):
    placed = (
        P("gx", "gy", None, None, None),
        P("gx", "gy", None, None, None),
        P(),
        P("gx", "gy", None),
        P("gx", "gy", None, None),
    )
    return jax.shard_map(
        on_device,
        mesh=mesh,
        in_specs=placed,
        out_specs=P("gx", "gy", None, None, None),
        check_vma=False,
    )
```

```python
import functools

import jax
import jax.numpy as jnp
import numpy as np
from jax import lax
from jax.experimental import pallas as pl
from jax.experimental.pallas import tpu as pltpu
from jax.sharding import PartitionSpec as P

VARS = 5
NODES = 5
SQUARE = NODES * NODES
FACE = VARS * SQUARE
BLOCK = FACE * NODES
LANE = 128
MESH = pl.DeviceIdType.MESH


def orient_table():
    table = np.zeros((8, LANE, LANE), np.float32)
    for orient in range(8):
        for variable in range(VARS):
            for first in range(NODES):
                for second in range(NODES):
                    p, q = (second, first) if orient & 1 else (first, second)
                    if orient & 2:
                        p = NODES - 1 - p
                    if orient & 4:
                        q = NODES - 1 - q
                    target = variable * SQUARE + first * NODES + second
                    table[orient, target, variable * SQUARE + p * NODES + q] = 1.0
    return table


def dot(a, b):
    return jnp.dot(a, b, preferred_element_type=jnp.float32)


def row_chunks(block):
    return [(start, min(LANE, block - start)) for start in range(0, block, LANE)]


def sweep_kernel(
    order, orient, table_hbm, lift_hbm, rhs_hbm, inv_hbm, sol,
    table, lift, raw_r, raw_b, stage, rhs, inv, padded, turned, plain, wide, weight, part, picked, trace_m, trace_r,
    begun, inc, out, load_sem, r_sem, b_sem, x_send, y_send, x_recv, y_recv,
):
    block, planes, columns = raw_r.shape
    parts = columns // LANE
    two, three = 2 * LANE, 3 * LANE
    chunks = row_chunks(block)
    tiles = [(t, min(LANE, block - t)) for t in range(0, block, LANE)]
    count_x, count_y = lax.axis_size("gx"), lax.axis_size("gy")
    me_x, me_y = lax.axis_index("gx"), lax.axis_index("gy")
    has_left, has_right = me_x > 0, me_x < count_x - 1
    has_below, has_above = me_y > 0, me_y < count_y - 1

    loads = [
        pltpu.make_async_copy(source, target, load_sem.at[i])
        for i, (source, target) in enumerate([(lift_hbm, lift), (table_hbm, table)])
    ]
    loads[0].start()

    def fetch(i, start, size):
        rows = pl.ds(start, size)
        return (
            pltpu.make_async_copy(rhs_hbm.at[rows], raw_r.at[rows], r_sem.at[i]),
            pltpu.make_async_copy(inv_hbm.at[rows], raw_b.at[rows], b_sem.at[i]),
        )

    whole = block // LANE
    depth = min(2, len(chunks))
    for i, (start, size) in list(enumerate(chunks))[:depth]:
        for copy in fetch(i, start, size):
            copy.start()
    loads[1].start()

    barrier = pltpu.get_barrier_semaphore()
    for present, x, y in (
        (has_left, me_x - 1, me_y),
        (has_right, me_x + 1, me_y),
        (has_below, me_x, me_y - 1),
        (has_above, me_x, me_y + 1),
    ):
        @pl.when(present)
        def _():
            pl.semaphore_signal(barrier, inc=1, device_id=(x, y), device_id_type=MESH)

    part[...] = jnp.zeros_like(part)
    out[0] = jnp.zeros(out.shape[1:], out.dtype)
    for d in range(3):
        tail = (d + 1) * LANE - 8
        trace_r[:, :, tail : tail + 8, :] = jnp.zeros((planes, parts, 8, LANE), trace_r.dtype)

    distance = me_x + me_y

    @pl.when(distance == 0)
    def _():
        trace_m[:, :, :two] = jnp.zeros((planes, three, two), trace_m.dtype)

    @pl.when(me_x == 0)
    def _():
        inc[:, :, :LANE, :] = jnp.zeros((planes, parts, LANE, LANE), inc.dtype)

    @pl.when(me_y == 0)
    def _():
        inc[:, :, LANE:, :] = jnp.zeros((planes, parts, LANE, LANE), inc.dtype)

    row = lax.broadcasted_iota(jnp.int32, (3 * FACE, three), 0)
    col = lax.broadcasted_iota(jnp.int32, (3 * FACE, three), 1)
    face = jnp.where(col >= two, 2, jnp.where(col >= LANE, 1, 0))
    inside = col - face * LANE
    spread = ((inside < FACE) & (row == face * FACE + inside)).astype(jnp.float32).astype(jnp.bfloat16)
    loads[0].wait()
    padded[...] = lax.dot_general(
        lift[...], spread, (((0,), (0,)), ((), ())), preferred_element_type=jnp.float32
    ).astype(jnp.bfloat16)

    def widen(raw, start, size, lanes, t):
        mixed = raw[pl.ds(start, size), :, lanes].astype(jnp.float32)
        rows = pl.ds(start * planes, size * planes)
        stage[t, rows, : mixed.shape[-1]] = mixed.reshape(size * planes, mixed.shape[-1])

    def arrange(i, start, size):
        for copy in fetch(i, start, size):
            copy.wait()
        if size == LANE:
            @pl.when(i + depth < whole)
            def _():
                for copy in fetch(i + depth, pl.multiple_of(start + depth * LANE, LANE), LANE):
                    copy.start()

            if whole < len(chunks):
                @pl.when(i + depth == whole)
                def _():
                    for copy in fetch(whole, *chunks[whole]):
                        copy.start()

        for t, (first, lanes) in enumerate(tiles):
            widen(raw_b, start, size, slice(first, first + lanes), t)
        for t in range(columns // LANE):
            widen(raw_r, start, size, slice(t * LANE, (t + 1) * LANE), len(tiles) + t)

    def arrange_full(i, carry):
        arrange(i, pl.multiple_of(i * LANE, LANE), LANE)
        return carry

    lax.fori_loop(0, whole, arrange_full, 0)
    for i, (start, size) in list(enumerate(chunks))[whole:]:
        arrange(i, start, size)
    loads[1].wait()

    def pick(source, put, first, step):
        def rows(start, size, stride=1):
            return source[pl.ds(first + start * step, size, stride=stride * step), :]

        for v in range(VARS):
            put(v * SQUARE, rows(v * FACE + FACE - SQUARE, SQUARE))
        for v in range(VARS * NODES):
            put(LANE + v * NODES, rows(v * SQUARE + SQUARE - NODES, NODES))
        put(two, rows(NODES - 1, FACE, NODES))

    def take_right(slot, into=0):
        for t in range(parts):
            rows = stage[len(tiles) + t, pl.ds(slot, block, stride=planes), :]
            rhs[into, :, t * LANE : (t + 1) * LANE] = rows.astype(jnp.bfloat16)

    def take_block(slot):
        for t, (first, lanes) in enumerate(tiles):
            rows = stage[t, pl.ds(slot, block, stride=planes), :]
            inv[:, first : first + lanes] = rows[:, :lanes].astype(jnp.bfloat16)

    def turn_into(k, d, moved, slot):
        turned_face = dot(moved.astype(jnp.bfloat16), table[orient[d, 0, slot]])
        trace_m[k, :, d * LANE : (d + 1) * LANE] = turned_face.astype(jnp.bfloat16)

    def prepare_traces(k, first_face, u=0):
        slot = order[k]
        for t, (first, lanes) in enumerate(tiles):
            def put_part(start, rows):
                part[u, t, pl.ds(start, rows.shape[0]), :] = rows

            pick(stage.at[t], put_part, slot, planes)
            picked[u, :, first : first + lanes] = part[u, t, :, :lanes].astype(jnp.bfloat16)
        take_right(slot, u)
        solved = dot(picked[u], rhs[u])
        for c in range(parts):
            trace_r[k, c] = solved[:, c * LANE : (c + 1) * LANE]
        moved = dot(picked[u], padded[:, first_face * LANE :])
        for d in range(first_face, 3):
            turn_into(k, d, moved[:, (d - first_face) * LANE : (d - first_face + 1) * LANE], slot)

    def prepare_all(k):
        slot = order[k]
        take_right(slot)
        take_block(slot)
        solved = dot(inv[...], rhs[0])
        for c in range(parts):
            plain[k, c] = solved[:, c * LANE : (c + 1) * LANE]

            def put_plain(start, rows):
                trace_r[k, c, pl.ds(start, rows.shape[0]), :] = rows

            pick(plain.at[k, c], put_plain, 0, 1)
        spreads = dot(inv[...], padded[...])
        weight[k] = spreads.astype(jnp.bfloat16)
        for d in range(3):
            wide[d] = spreads[:, d * LANE : (d + 1) * LANE]

            def put_part(start, rows):
                part[0, d, pl.ds(start, rows.shape[0]), :] = rows

            pick(wide.at[d], put_part, 0, 1)
            turn_into(k, d, part[0, d], slot)

    def hop(k, c, axis):
        rows = pl.ds(axis * LANE, LANE)
        send, recv = ((x_send, x_recv), (y_send, y_recv))[axis]
        return pltpu.make_async_remote_copy(
            src_ref=out.at[k + 1, c, rows, :],
            dst_ref=inc.at[k, c, rows, :],
            send_sem=send.at[k, c],
            recv_sem=recv.at[k, c],
            device_id=((me_x + 1, me_y), (me_x, me_y + 1))[axis],
            device_id_type=MESH,
        )

    def advance(k, c):
        @pl.when(has_left)
        def _():
            hop(k, c, 0).wait_recv()

        @pl.when(has_below)
        def _():
            hop(k, c, 1).wait_recv()

        gone = dot(trace_m[k, :two, :two], inc[k, c])
        out[k + 1, c, :two, :] = (begun[c, :two, :] - gone).astype(jnp.bfloat16)

        @pl.when(has_above)
        def _():
            hop(k, c, 1).start()

        @pl.when(has_right)
        def _():
            hop(k, c, 0).start()

    def follow(k):
        arrived = jnp.concatenate([inc[k, c] for c in range(parts)], axis=-1)
        gone = dot(trace_m[k, two:, :two], arrived)
        rising = [
            (begun[c, two:, :] - gone[:, c * LANE : (c + 1) * LANE]).astype(jnp.bfloat16) for c in range(parts)
        ]
        later = jnp.minimum(k + 1, planes - 1)
        lifted = dot(trace_m[later, :, two:], jnp.concatenate(rising, axis=-1))
        for c in range(parts):
            out[k + 1, c, two:, :] = rising[c]
            begun[c] = trace_r[later, c] - lifted[:, c * LANE : (c + 1) * LANE]

    def turn_faces(k, slot):
        faces = [[inc[k, c, d * LANE : (d + 1) * LANE, :] for c in range(parts)] for d in range(2)]
        faces.append([out[k, c, two:, :] for c in range(parts)])
        for d in range(3):
            face = jnp.concatenate(faces[d], axis=-1)
            turned[d * LANE : (d + 1) * LANE, :] = dot(table[orient[d, 0, slot]], face).astype(jnp.bfloat16)

    def finish_late(k):
        slot = order[k]
        take_block(slot)
        turn_faces(k, slot)
        lifted = dot(padded[...], turned[...])
        for t in range(parts):
            rows = stage[len(tiles) + t, pl.ds(slot, block, stride=planes), :]
            rhs[0, :, t * LANE : (t + 1) * LANE] = (rows - lifted[:, t * LANE : (t + 1) * LANE]).astype(jnp.bfloat16)
        swept = dot(inv[...], rhs[0])
        for c in range(parts):
            sol[c, pl.ds(k, block, stride=planes), :] = swept[:, c * LANE : (c + 1) * LANE]

    def finish(k):
        turn_faces(k, order[k])
        lifted = dot(weight[k], turned[...])
        for c in range(parts):
            sol[c, pl.ds(k, block, stride=planes), :] = plain[k, c] - lifted[:, c * LANE : (c + 1) * LANE]

    near = distance * 5 <= (count_x + count_y - 2) * 2
    neighbours = sum(p.astype(jnp.int32) for p in (has_left, has_right, has_below, has_above))

    def loop(start, stop, *works):
        def body(k, carry):
            for work in works:
                work(k)
            return carry

        lax.fori_loop(start, stop, body, 0)

    def advances(k):
        for c in range(parts):
            advance(k, c)

    def enter():
        pl.semaphore_wait(barrier, neighbours)
        begun[...] = trace_r[0]

    def prepare_pair(k):
        for u in range(2):
            prepare_traces(2 * k + u, 0, u)

    @pl.when(distance == 0)
    def _():
        prepare_traces(0, 2)
        enter()
        loop(0, planes - 1, advances, lambda k: prepare_traces(k + 1, 2), follow)
        loop(planes - 1, planes, advances, follow)

    early = (distance > 0) & (distance * 10 <= (count_x + count_y - 2) * 3)

    @pl.when(early)
    def _():
        loop(0, planes // 4, prepare_pair)
        enter()

        def two_steps(j):
            advances(2 * j)
            prepare_traces(2 * (planes // 4) + j, 0)
            follow(2 * j)
            advances(2 * j + 1)
            follow(2 * j + 1)

        loop(0, planes // 2, two_steps)

    @pl.when(near & (distance > 0) & jnp.logical_not(early))
    def _():
        loop(0, planes // 2, prepare_pair)
        enter()
        loop(0, planes, advances, follow)

    @pl.when(near)
    def _():
        loop(0, planes, finish_late)

    @pl.when(jnp.logical_not(near))
    def _():
        loop(0, planes, prepare_all)
        enter()
        loop(0, planes, advances, follow, finish)

    def drain(k, carry):
        for c in range(parts):
            @pl.when(has_right)
            def _():
                hop(k, c, 0).wait_send()

            @pl.when(has_above)
            def _():
                hop(k, c, 1).wait_send()
        return carry

    lax.fori_loop(0, planes, drain, 0)


def place_kernel(order, sol, out, ready, sems):
    block, planes, columns = ready.shape
    chunks = row_chunks(block)
    whole = block // LANE
    place_of = lax.broadcasted_iota(jnp.int32, (planes, LANE), 0)
    source = jnp.zeros((planes, LANE), jnp.int32)
    for k in range(planes):
        source = jnp.where(place_of == order[k], k, source)

    def put(i, start, size):
        rows = pl.ds(start, size)
        return pltpu.make_async_copy(ready.at[rows], out.at[rows], sems.at[i])

    def place(i, start, size):
        rows = pl.ds(start, size)
        picks = jnp.broadcast_to(source[None], (size, planes, LANE))
        for t in range(columns // LANE):
            lanes = slice(t * LANE, (t + 1) * LANE)
            swept = sol[t, pl.ds(start * planes, size * planes), :].reshape(size, planes, LANE)
            placed = jnp.take_along_axis(swept, picks, axis=1, mode="promise_in_bounds")
            ready[rows, :, lanes] = placed.astype(jnp.bfloat16)
        put(i, start, size).start()

    def place_full(i, carry):
        place(i, pl.multiple_of(i * LANE, LANE), LANE)
        return carry

    lax.fori_loop(0, whole, place_full, 0)
    for i, (start, size) in list(enumerate(chunks))[whole:]:
        place(i, start, size)
    for i, (start, size) in enumerate(chunks):
        put(i, start, size).wait()


def on_device(right_side, inverse_blocks, lift_matrix, plane_order, face_orient):
    rhs = jnp.transpose(right_side, (0, 1, 3, 2, 4))[0, 0]
    inv = jnp.transpose(inverse_blocks, (0, 1, 3, 2, 4))[0, 0]
    order = plane_order[0, 0]
    orient = jnp.transpose(face_orient, (0, 3, 1, 2))[0]
    block, planes, columns = rhs.shape
    tiles = pl.cdiv(block, LANE)
    chunks = len(row_chunks(block))
    parts = columns // LANE
    two, three = 2 * LANE, 3 * LANE
    bf16, f32 = jnp.bfloat16, jnp.float32
    table = jnp.asarray(orient_table(), bf16)
    lift = lift_matrix.T
    smem = pl.BlockSpec(memory_space=pltpu.SMEM)
    vmem = pl.BlockSpec(memory_space=pltpu.VMEM)
    anywhere = pl.BlockSpec(memory_space=pl.ANY)
    sol = pl.pallas_call(
        sweep_kernel,
        out_shape=pltpu.VMEM((parts, block * planes, LANE), f32),
        in_specs=[smem, smem] + [anywhere] * 4,
        out_specs=vmem,
        scratch_shapes=[
            pltpu.VMEM(table.shape, bf16),
            pltpu.VMEM(lift.shape, bf16),
            pltpu.VMEM(rhs.shape, bf16),
            pltpu.VMEM(inv.shape, bf16),
            pltpu.VMEM((tiles + parts, block * planes, LANE), f32),
            pltpu.VMEM((2, block, columns), bf16),
            pltpu.VMEM((block, block), bf16),
            pltpu.VMEM((block, three), bf16),
            pltpu.VMEM((three, columns), bf16),
            pltpu.VMEM((planes, parts, block, LANE), f32),
            pltpu.VMEM((3, block, LANE), f32),
            pltpu.VMEM((planes, block, three), bf16),
            pltpu.VMEM((2, max(tiles, 3), three, LANE), f32),
            pltpu.VMEM((2, three, block), bf16),
            pltpu.VMEM((planes, three, three), bf16),
            pltpu.VMEM((planes, parts, three, LANE), f32),
            pltpu.VMEM((parts, three, LANE), f32),
            pltpu.VMEM((planes, parts, two, LANE), bf16),
            pltpu.VMEM((planes + 1, parts, three, LANE), bf16),
            pltpu.SemaphoreType.DMA((2,)),
            pltpu.SemaphoreType.DMA((chunks,)),
            pltpu.SemaphoreType.DMA((chunks,)),
            pltpu.SemaphoreType.DMA((planes, parts)),
            pltpu.SemaphoreType.DMA((planes, parts)),
            pltpu.SemaphoreType.DMA((planes, parts)),
            pltpu.SemaphoreType.DMA((planes, parts)),
        ],
        compiler_params=pltpu.CompilerParams(
            collective_id=0, has_side_effects=True, vmem_limit_bytes=57 * 1024 * 1024
        ),
    )(order, orient, table, lift, rhs, inv)
    result = pl.pallas_call(
        place_kernel,
        out_shape=jax.ShapeDtypeStruct(rhs.shape, bf16),
        in_specs=[smem, vmem],
        out_specs=anywhere,
        scratch_shapes=[
            pltpu.VMEM(rhs.shape, bf16),
            pltpu.SemaphoreType.DMA((chunks,)),
        ],
        compiler_params=pltpu.CompilerParams(vmem_limit_bytes=16 * 1024 * 1024),
    )(order, sol)
    return jnp.transpose(result[None, None], (0, 1, 3, 2, 4))


def solution(mesh):
    placed = (
        P("gx", "gy", None, None, None),
        P("gx", "gy", None, None, None),
        P(),
        P("gx", "gy", None),
        P("gx", "gy", None, None),
    )
    return jax.shard_map(
        on_device,
        mesh=mesh,
        in_specs=placed,
        out_specs=P("gx", "gy", None, None, None),
        check_vma=False,
    )
```

```python
import functools

import jax
import jax.numpy as jnp
import numpy as np
from jax import lax
from jax.experimental import pallas as pl
from jax.experimental.pallas import tpu as pltpu
from jax.sharding import PartitionSpec as P

VARS = 5
NODES = 5
SQUARE = NODES * NODES
FACE = VARS * SQUARE
BLOCK = FACE * NODES
LANE = 128
MESH = pl.DeviceIdType.MESH


def orient_table():
    table = np.zeros((8, LANE, LANE), np.float32)
    for orient in range(8):
        for variable in range(VARS):
            for first in range(NODES):
                for second in range(NODES):
                    p, q = (second, first) if orient & 1 else (first, second)
                    if orient & 2:
                        p = NODES - 1 - p
                    if orient & 4:
                        q = NODES - 1 - q
                    target = variable * SQUARE + first * NODES + second
                    table[orient, target, variable * SQUARE + p * NODES + q] = 1.0
    return table


def dot(a, b):
    return jnp.dot(a, b, preferred_element_type=jnp.float32)


def row_chunks(block):
    return [(start, min(LANE, block - start)) for start in range(0, block, LANE)]


def sweep_kernel(
    order, orient, table_hbm, lift_hbm, rhs_hbm, inv_hbm, sol,
    table, lift, raw_r, raw_b, stage, rhs, inv, padded, turned, plain, wide, weight, part, picked, trace_m, trace_r,
    begun, inc, out, load_sem, r_sem, b_sem, x_send, y_send, x_recv, y_recv,
):
    block, planes, columns = raw_r.shape
    parts = columns // LANE
    two, three = 2 * LANE, 3 * LANE
    chunks = row_chunks(block)
    tiles = [(t, min(LANE, block - t)) for t in range(0, block, LANE)]
    count_x, count_y = lax.axis_size("gx"), lax.axis_size("gy")
    me_x, me_y = lax.axis_index("gx"), lax.axis_index("gy")
    has_left, has_right = me_x > 0, me_x < count_x - 1
    has_below, has_above = me_y > 0, me_y < count_y - 1

    loads = [
        pltpu.make_async_copy(source, target, load_sem.at[i])
        for i, (source, target) in enumerate([(lift_hbm, lift), (table_hbm, table)])
    ]
    loads[0].start()

    def fetch(i, start, size):
        rows = pl.ds(start, size)
        return (
            pltpu.make_async_copy(rhs_hbm.at[rows], raw_r.at[rows], r_sem.at[i]),
            pltpu.make_async_copy(inv_hbm.at[rows], raw_b.at[rows], b_sem.at[i]),
        )

    whole = block // LANE
    depth = min(3, len(chunks))
    for i, (start, size) in list(enumerate(chunks))[:depth]:
        for copy in fetch(i, start, size):
            copy.start()
    loads[1].start()

    barrier = pltpu.get_barrier_semaphore()
    for present, x, y in (
        (has_left, me_x - 1, me_y),
        (has_right, me_x + 1, me_y),
        (has_below, me_x, me_y - 1),
        (has_above, me_x, me_y + 1),
    ):
        @pl.when(present)
        def _():
            pl.semaphore_signal(barrier, inc=1, device_id=(x, y), device_id_type=MESH)

    part[...] = jnp.zeros_like(part)
    out[0] = jnp.zeros(out.shape[1:], out.dtype)
    for d in range(3):
        tail = (d + 1) * LANE - 8
        trace_r[:, :, tail : tail + 8, :] = jnp.zeros((planes, parts, 8, LANE), trace_r.dtype)

    distance = me_x + me_y

    @pl.when(me_x == 0)
    def _():
        inc[:, :, :LANE, :] = jnp.zeros((planes, parts, LANE, LANE), inc.dtype)

    @pl.when(me_y == 0)
    def _():
        inc[:, :, LANE:, :] = jnp.zeros((planes, parts, LANE, LANE), inc.dtype)

    row = lax.broadcasted_iota(jnp.int32, (3 * FACE, three), 0)
    col = lax.broadcasted_iota(jnp.int32, (3 * FACE, three), 1)
    face = jnp.where(col >= two, 2, jnp.where(col >= LANE, 1, 0))
    inside = col - face * LANE
    spread = ((inside < FACE) & (row == face * FACE + inside)).astype(jnp.float32).astype(jnp.bfloat16)
    loads[0].wait()
    padded[...] = lax.dot_general(
        lift[...], spread, (((0,), (0,)), ((), ())), preferred_element_type=jnp.float32
    ).astype(jnp.bfloat16)

    def widen(raw, start, size, lanes, t):
        mixed = raw[pl.ds(start, size), :, lanes].astype(jnp.float32)
        rows = pl.ds(start * planes, size * planes)
        stage[t, rows, : mixed.shape[-1]] = mixed.reshape(size * planes, mixed.shape[-1])

    def arrange(i, start, size):
        for copy in fetch(i, start, size):
            copy.wait()
        if size == LANE:
            @pl.when(i + depth < whole)
            def _():
                for copy in fetch(i + depth, pl.multiple_of(start + depth * LANE, LANE), LANE):
                    copy.start()

            if whole < len(chunks):
                @pl.when(i + depth == whole)
                def _():
                    for copy in fetch(whole, *chunks[whole]):
                        copy.start()

        for t, (first, lanes) in enumerate(tiles):
            widen(raw_b, start, size, slice(first, first + lanes), t)
        for t in range(columns // LANE):
            widen(raw_r, start, size, slice(t * LANE, (t + 1) * LANE), len(tiles) + t)

    def arrange_full(i, carry):
        arrange(i, pl.multiple_of(i * LANE, LANE), LANE)
        return carry

    lax.fori_loop(0, whole, arrange_full, 0)
    for i, (start, size) in list(enumerate(chunks))[whole:]:
        arrange(i, start, size)
    loads[1].wait()

    def pick(source, put, first, step):
        def rows(start, size, stride=1):
            return source[pl.ds(first + start * step, size, stride=stride * step), :]

        for v in range(VARS):
            put(v * SQUARE, rows(v * FACE + FACE - SQUARE, SQUARE))
        for v in range(VARS * NODES):
            put(LANE + v * NODES, rows(v * SQUARE + SQUARE - NODES, NODES))
        put(two, rows(NODES - 1, FACE, NODES))

    def take_right(slot, into=0):
        for t in range(parts):
            rows = stage[len(tiles) + t, pl.ds(slot, block, stride=planes), :]
            rhs[into, :, t * LANE : (t + 1) * LANE] = rows.astype(jnp.bfloat16)

    def take_block(slot):
        for t, (first, lanes) in enumerate(tiles):
            rows = stage[t, pl.ds(slot, block, stride=planes), :]
            inv[:, first : first + lanes] = rows[:, :lanes].astype(jnp.bfloat16)

    def turn_into(k, d, moved, slot):
        turned_face = dot(moved.astype(jnp.bfloat16), table[orient[d, 0, slot]])
        trace_m[k, :, d * LANE : (d + 1) * LANE] = turned_face.astype(jnp.bfloat16)

    def gather(k, u=0):
        slot = order[k]
        for t, (first, lanes) in enumerate(tiles):
            def put_part(start, rows):
                part[u, t, pl.ds(start, rows.shape[0]), :] = rows

            pick(stage.at[t], put_part, slot, planes)
            picked[u, :, first : first + lanes] = part[u, t, :, :lanes].astype(jnp.bfloat16)
        take_right(slot, u)

    def solve(k, first_face, u=0):
        slot = order[k]
        solved = dot(picked[u], rhs[u])
        for c in range(parts):
            trace_r[k, c] = solved[:, c * LANE : (c + 1) * LANE]
        moved = dot(picked[u], padded[:, first_face * LANE :])
        for d in range(first_face, 3):
            turn_into(k, d, moved[:, (d - first_face) * LANE : (d - first_face + 1) * LANE], slot)

    def prepare_all(k):
        slot = order[k]
        take_right(slot)
        take_block(slot)
        solved = dot(inv[...], rhs[0])
        for c in range(parts):
            plain[k, c] = solved[:, c * LANE : (c + 1) * LANE]

            def put_plain(start, rows):
                trace_r[k, c, pl.ds(start, rows.shape[0]), :] = rows

            pick(plain.at[k, c], put_plain, 0, 1)
        spreads = dot(inv[...], padded[...])
        weight[k] = spreads.astype(jnp.bfloat16)
        for d in range(3):
            wide[d] = spreads[:, d * LANE : (d + 1) * LANE]

            def put_part(start, rows):
                part[0, d, pl.ds(start, rows.shape[0]), :] = rows

            pick(wide.at[d], put_part, 0, 1)
            turn_into(k, d, part[0, d], slot)

    def hop(k, c, axis):
        rows = pl.ds(axis * LANE, LANE)
        send, recv = ((x_send, x_recv), (y_send, y_recv))[axis]
        return pltpu.make_async_remote_copy(
            src_ref=out.at[k + 1, c, rows, :],
            dst_ref=inc.at[k, c, rows, :],
            send_sem=send.at[k, c],
            recv_sem=recv.at[k, c],
            device_id=((me_x + 1, me_y), (me_x, me_y + 1))[axis],
            device_id_type=MESH,
        )

    def advance(k, c):
        @pl.when(has_left)
        def _():
            hop(k, c, 0).wait_recv()

        @pl.when(has_below)
        def _():
            hop(k, c, 1).wait_recv()

        gone = dot(trace_m[k, :two, :two], inc[k, c])
        out[k + 1, c, :two, :] = (begun[c, :two, :] - gone).astype(jnp.bfloat16)
        send(k, c)

    def send(k, c):
        @pl.when(has_above)
        def _():
            hop(k, c, 1).start()

        @pl.when(has_right)
        def _():
            hop(k, c, 0).start()

    def follow(k):
        arrived = jnp.concatenate([inc[k, c] for c in range(parts)], axis=-1)
        gone = dot(trace_m[k, two:, :two], arrived)
        rising = [
            (begun[c, two:, :] - gone[:, c * LANE : (c + 1) * LANE]).astype(jnp.bfloat16) for c in range(parts)
        ]
        later = jnp.minimum(k + 1, planes - 1)
        lifted = dot(trace_m[later, :, two:], jnp.concatenate(rising, axis=-1))
        for c in range(parts):
            out[k + 1, c, two:, :] = rising[c]
            begun[c] = trace_r[later, c] - lifted[:, c * LANE : (c + 1) * LANE]

    def corner_sends(k):
        for c in range(parts):
            out[k + 1, c] = begun[c].astype(jnp.bfloat16)
        for c in range(parts):
            send(k, c)

    def corner_follow(k):
        rising = jnp.concatenate([begun[c, two:, :] for c in range(parts)], axis=-1).astype(jnp.bfloat16)
        later = jnp.minimum(k + 1, planes - 1)
        lifted = dot(trace_m[later, :, two:], rising)
        for c in range(parts):
            begun[c] = trace_r[later, c] - lifted[:, c * LANE : (c + 1) * LANE]

    def turn_faces(k, slot):
        faces = [[inc[k, c, d * LANE : (d + 1) * LANE, :] for c in range(parts)] for d in range(2)]
        faces.append([out[k, c, two:, :] for c in range(parts)])
        for d in range(3):
            face = jnp.concatenate(faces[d], axis=-1)
            turned[d * LANE : (d + 1) * LANE, :] = dot(table[orient[d, 0, slot]], face).astype(jnp.bfloat16)

    def finish_late(k):
        slot = order[k]
        take_block(slot)
        turn_faces(k, slot)
        lifted = dot(padded[...], turned[...])
        for t in range(parts):
            rows = stage[len(tiles) + t, pl.ds(slot, block, stride=planes), :]
            rhs[0, :, t * LANE : (t + 1) * LANE] = (rows - lifted[:, t * LANE : (t + 1) * LANE]).astype(jnp.bfloat16)
        swept = dot(inv[...], rhs[0])
        for c in range(parts):
            sol[c, pl.ds(k, block, stride=planes), :] = swept[:, c * LANE : (c + 1) * LANE]

    def finish(k):
        turn_faces(k, order[k])
        lifted = dot(weight[k], turned[...])
        for c in range(parts):
            sol[c, pl.ds(k, block, stride=planes), :] = plain[k, c] - lifted[:, c * LANE : (c + 1) * LANE]

    near = distance * 5 <= (count_x + count_y - 2) * 2
    neighbours = sum(p.astype(jnp.int32) for p in (has_left, has_right, has_below, has_above))

    def loop(start, stop, *works):
        def body(k, carry):
            for work in works:
                work(k)
            return carry

        lax.fori_loop(start, stop, body, 0)

    def advances(k):
        for c in range(parts):
            advance(k, c)

    def enter():
        pl.semaphore_wait(barrier, neighbours)
        begun[...] = trace_r[0]

    def prepare_pair(k):
        for u in range(2):
            gather(2 * k + u, u)
            solve(2 * k + u, 0, u)

    @pl.when(distance == 0)
    def _():
        last = planes - 1
        gather(0, 0)
        solve(0, 2, 0)
        enter()

        def two_steps(j):
            corner_sends(2 * j)

            @pl.when(j == 0)
            def _():
                gather(1, 1)

            solve(2 * j + 1, 2, 1)
            gather(jnp.minimum(2 * j + 2, last), 0)
            corner_follow(2 * j)
            corner_sends(2 * j + 1)
            solve(jnp.minimum(2 * j + 2, last), 2, 0)
            gather(jnp.minimum(2 * j + 3, last), 1)
            corner_follow(2 * j + 1)

        loop(0, planes // 2, two_steps)

    early = (distance > 0) & (distance * 10 <= (count_x + count_y - 2) * 3)

    @pl.when(early)
    def _():
        half = planes // 2
        loop(0, half // 2, prepare_pair)
        gather(half)
        enter()

        def two_steps(j):
            advances(2 * j)
            solve(half + j, 0)
            follow(2 * j)
            advances(2 * j + 1)
            gather(jnp.minimum(half + 1 + j, planes - 1))
            follow(2 * j + 1)

        loop(0, half, two_steps)

    @pl.when(near & (distance > 0) & jnp.logical_not(early))
    def _():
        loop(0, planes // 2, prepare_pair)
        enter()
        loop(0, planes, advances, follow)

    @pl.when(near)
    def _():
        loop(0, planes, finish_late)

    @pl.when(jnp.logical_not(near))
    def _():
        loop(0, planes, prepare_all)
        enter()
        loop(0, planes, advances, follow, finish)

    def drain(k, carry):
        for c in range(parts):
            @pl.when(has_right)
            def _():
                hop(k, c, 0).wait_send()

            @pl.when(has_above)
            def _():
                hop(k, c, 1).wait_send()
        return carry

    lax.fori_loop(0, planes, drain, 0)


def place_kernel(order, sol, out, ready, sems):
    block, planes, columns = ready.shape
    chunks = row_chunks(block)
    whole = block // LANE
    place_of = lax.broadcasted_iota(jnp.int32, (planes, LANE), 0)
    source = jnp.zeros((planes, LANE), jnp.int32)
    for k in range(planes):
        source = jnp.where(place_of == order[k], k, source)

    def put(i, start, size):
        rows = pl.ds(start, size)
        return pltpu.make_async_copy(ready.at[rows], out.at[rows], sems.at[i])

    def place(i, start, size):
        rows = pl.ds(start, size)
        picks = jnp.broadcast_to(source[None], (size, planes, LANE))
        for t in range(columns // LANE):
            lanes = slice(t * LANE, (t + 1) * LANE)
            swept = sol[t, pl.ds(start * planes, size * planes), :].reshape(size, planes, LANE)
            placed = jnp.take_along_axis(swept, picks, axis=1, mode="promise_in_bounds")
            ready[rows, :, lanes] = placed.astype(jnp.bfloat16)
        put(i, start, size).start()

    def place_full(i, carry):
        place(i, pl.multiple_of(i * LANE, LANE), LANE)
        return carry

    lax.fori_loop(0, whole, place_full, 0)
    for i, (start, size) in list(enumerate(chunks))[whole:]:
        place(i, start, size)
    for i, (start, size) in enumerate(chunks):
        put(i, start, size).wait()


def on_device(right_side, inverse_blocks, lift_matrix, plane_order, face_orient):
    rhs = jnp.transpose(right_side, (0, 1, 3, 2, 4))[0, 0]
    inv = jnp.transpose(inverse_blocks, (0, 1, 3, 2, 4))[0, 0]
    order = plane_order[0, 0]
    orient = jnp.transpose(face_orient, (0, 3, 1, 2))[0]
    block, planes, columns = rhs.shape
    tiles = pl.cdiv(block, LANE)
    chunks = len(row_chunks(block))
    parts = columns // LANE
    two, three = 2 * LANE, 3 * LANE
    bf16, f32 = jnp.bfloat16, jnp.float32
    table = jnp.asarray(orient_table(), bf16)
    lift = lift_matrix.T
    smem = pl.BlockSpec(memory_space=pltpu.SMEM)
    vmem = pl.BlockSpec(memory_space=pltpu.VMEM)
    anywhere = pl.BlockSpec(memory_space=pl.ANY)
    sol = pl.pallas_call(
        sweep_kernel,
        out_shape=pltpu.VMEM((parts, block * planes, LANE), f32),
        in_specs=[smem, smem] + [anywhere] * 4,
        out_specs=vmem,
        scratch_shapes=[
            pltpu.VMEM(table.shape, bf16),
            pltpu.VMEM(lift.shape, bf16),
            pltpu.VMEM(rhs.shape, bf16),
            pltpu.VMEM(inv.shape, bf16),
            pltpu.VMEM((tiles + parts, block * planes, LANE), f32),
            pltpu.VMEM((2, block, columns), bf16),
            pltpu.VMEM((block, block), bf16),
            pltpu.VMEM((block, three), bf16),
            pltpu.VMEM((three, columns), bf16),
            pltpu.VMEM((planes, parts, block, LANE), f32),
            pltpu.VMEM((3, block, LANE), f32),
            pltpu.VMEM((planes, block, three), bf16),
            pltpu.VMEM((2, max(tiles, 3), three, LANE), f32),
            pltpu.VMEM((2, three, block), bf16),
            pltpu.VMEM((planes, three, three), bf16),
            pltpu.VMEM((planes, parts, three, LANE), f32),
            pltpu.VMEM((parts, three, LANE), f32),
            pltpu.VMEM((planes, parts, two, LANE), bf16),
            pltpu.VMEM((planes + 1, parts, three, LANE), bf16),
            pltpu.SemaphoreType.DMA((2,)),
            pltpu.SemaphoreType.DMA((chunks,)),
            pltpu.SemaphoreType.DMA((chunks,)),
            pltpu.SemaphoreType.DMA((planes, parts)),
            pltpu.SemaphoreType.DMA((planes, parts)),
            pltpu.SemaphoreType.DMA((planes, parts)),
            pltpu.SemaphoreType.DMA((planes, parts)),
        ],
        compiler_params=pltpu.CompilerParams(
            collective_id=0, has_side_effects=True, vmem_limit_bytes=57 * 1024 * 1024
        ),
    )(order, orient, table, lift, rhs, inv)
    result = pl.pallas_call(
        place_kernel,
        out_shape=jax.ShapeDtypeStruct(rhs.shape, bf16),
        in_specs=[smem, vmem],
        out_specs=anywhere,
        scratch_shapes=[
            pltpu.VMEM(rhs.shape, bf16),
            pltpu.SemaphoreType.DMA((chunks,)),
        ],
        compiler_params=pltpu.CompilerParams(vmem_limit_bytes=16 * 1024 * 1024),
    )(order, sol)
    return jnp.transpose(result[None, None], (0, 1, 3, 2, 4))


def solution(mesh):
    placed = (
        P("gx", "gy", None, None, None),
        P("gx", "gy", None, None, None),
        P(),
        P("gx", "gy", None),
        P("gx", "gy", None, None),
    )
    return jax.shard_map(
        on_device,
        mesh=mesh,
        in_specs=placed,
        out_specs=P("gx", "gy", None, None, None),
        check_vma=False,
    )
```

```python
import functools

import jax
import jax.numpy as jnp
import numpy as np
from jax import lax
from jax.experimental import pallas as pl
from jax.experimental.pallas import tpu as pltpu
from jax.sharding import PartitionSpec as P

VARS = 5
NODES = 5
SQUARE = NODES * NODES
FACE = VARS * SQUARE
BLOCK = FACE * NODES
LANE = 128
MESH = pl.DeviceIdType.MESH


def orient_table():
    table = np.zeros((8, LANE, LANE), np.float32)
    for orient in range(8):
        for variable in range(VARS):
            for first in range(NODES):
                for second in range(NODES):
                    p, q = (second, first) if orient & 1 else (first, second)
                    if orient & 2:
                        p = NODES - 1 - p
                    if orient & 4:
                        q = NODES - 1 - q
                    target = variable * SQUARE + first * NODES + second
                    table[orient, target, variable * SQUARE + p * NODES + q] = 1.0
    return table


def dot(a, b):
    return jnp.dot(a, b, preferred_element_type=jnp.float32)


def row_chunks(block):
    return [(start, min(LANE, block - start)) for start in range(0, block, LANE)]


def sweep_kernel(
    order, orient, table_hbm, lift_hbm, rhs_hbm, inv_hbm, sol,
    table, lift, raw_r, raw_b, stage, rhs, inv, padded, turned, plain, wide, weight, part, picked, trace_m, trace_r,
    begun, inc, out, load_sem, r_sem, b_sem, x_send, y_send, x_recv, y_recv,
):
    block, planes, columns = raw_r.shape
    parts = columns // LANE
    two, three = 2 * LANE, 3 * LANE
    chunks = row_chunks(block)
    tiles = [(t, min(LANE, block - t)) for t in range(0, block, LANE)]
    count_x, count_y = lax.axis_size("gx"), lax.axis_size("gy")
    me_x, me_y = lax.axis_index("gx"), lax.axis_index("gy")
    has_left, has_right = me_x > 0, me_x < count_x - 1
    has_below, has_above = me_y > 0, me_y < count_y - 1

    loads = [
        pltpu.make_async_copy(source, target, load_sem.at[i])
        for i, (source, target) in enumerate([(lift_hbm, lift), (table_hbm, table)])
    ]
    loads[0].start()

    def fetch(i, start, size):
        rows = pl.ds(start, size)
        return (
            pltpu.make_async_copy(rhs_hbm.at[rows], raw_r.at[rows], r_sem.at[i]),
            pltpu.make_async_copy(inv_hbm.at[rows], raw_b.at[rows], b_sem.at[i]),
        )

    whole = block // LANE
    depth = min(3, len(chunks))
    for i, (start, size) in list(enumerate(chunks))[:depth]:
        for copy in fetch(i, start, size):
            copy.start()
    loads[1].start()

    barrier = pltpu.get_barrier_semaphore()
    for present, x, y in (
        (has_left, me_x - 1, me_y),
        (has_right, me_x + 1, me_y),
        (has_below, me_x, me_y - 1),
        (has_above, me_x, me_y + 1),
    ):
        @pl.when(present)
        def _():
            pl.semaphore_signal(barrier, inc=1, device_id=(x, y), device_id_type=MESH)

    part[...] = jnp.zeros_like(part)
    out[0] = jnp.zeros(out.shape[1:], out.dtype)
    for d in range(3):
        tail = (d + 1) * LANE - 8
        trace_r[:, :, tail : tail + 8, :] = jnp.zeros((planes, parts, 8, LANE), trace_r.dtype)

    distance = me_x + me_y

    @pl.when(me_x == 0)
    def _():
        inc[:, :, :LANE, :] = jnp.zeros((planes, parts, LANE, LANE), inc.dtype)

    @pl.when(me_y == 0)
    def _():
        inc[:, :, LANE:, :] = jnp.zeros((planes, parts, LANE, LANE), inc.dtype)

    row = lax.broadcasted_iota(jnp.int32, (3 * FACE, three), 0)
    col = lax.broadcasted_iota(jnp.int32, (3 * FACE, three), 1)
    face = jnp.where(col >= two, 2, jnp.where(col >= LANE, 1, 0))
    inside = col - face * LANE
    spread = ((inside < FACE) & (row == face * FACE + inside)).astype(jnp.float32).astype(jnp.bfloat16)
    loads[0].wait()
    padded[...] = lax.dot_general(
        lift[...], spread, (((0,), (0,)), ((), ())), preferred_element_type=jnp.float32
    ).astype(jnp.bfloat16)

    def widen(raw, start, size, lanes, t):
        mixed = raw[pl.ds(start, size), :, lanes].astype(jnp.float32)
        rows = pl.ds(start * planes, size * planes)
        stage[t, rows, : mixed.shape[-1]] = mixed.reshape(size * planes, mixed.shape[-1])

    def arrange(i, start, size):
        for copy in fetch(i, start, size):
            copy.wait()
        if size == LANE:
            @pl.when(i + depth < whole)
            def _():
                for copy in fetch(i + depth, pl.multiple_of(start + depth * LANE, LANE), LANE):
                    copy.start()

            if whole < len(chunks):
                @pl.when(i + depth == whole)
                def _():
                    for copy in fetch(whole, *chunks[whole]):
                        copy.start()

        for t, (first, lanes) in enumerate(tiles):
            widen(raw_b, start, size, slice(first, first + lanes), t)
        for t in range(columns // LANE):
            widen(raw_r, start, size, slice(t * LANE, (t + 1) * LANE), len(tiles) + t)

    def arrange_full(i, carry):
        arrange(i, pl.multiple_of(i * LANE, LANE), LANE)
        return carry

    lax.fori_loop(0, whole, arrange_full, 0)
    for i, (start, size) in list(enumerate(chunks))[whole:]:
        arrange(i, start, size)
    loads[1].wait()

    def pick(source, put, first, step):
        def rows(start, size, stride=1):
            return source[pl.ds(first + start * step, size, stride=stride * step), :]

        for v in range(VARS):
            put(v * SQUARE, rows(v * FACE + FACE - SQUARE, SQUARE))
        for v in range(VARS * NODES):
            put(LANE + v * NODES, rows(v * SQUARE + SQUARE - NODES, NODES))
        put(two, rows(NODES - 1, FACE, NODES))

    def take_right(slot, into=0):
        for t in range(parts):
            rows = stage[len(tiles) + t, pl.ds(slot, block, stride=planes), :]
            rhs[into, :, t * LANE : (t + 1) * LANE] = rows.astype(jnp.bfloat16)

    def take_block(slot):
        for t, (first, lanes) in enumerate(tiles):
            rows = stage[t, pl.ds(slot, block, stride=planes), :]
            inv[:, first : first + lanes] = rows[:, :lanes].astype(jnp.bfloat16)

    def turn_into(k, d, moved, slot):
        turned_face = dot(moved.astype(jnp.bfloat16), table[orient[d, 0, slot]])
        trace_m[k, :, d * LANE : (d + 1) * LANE] = turned_face.astype(jnp.bfloat16)

    def gather(k, u=0):
        slot = order[k]
        for t, (first, lanes) in enumerate(tiles):
            def put_part(start, rows):
                part[u, t, pl.ds(start, rows.shape[0]), :] = rows

            pick(stage.at[t], put_part, slot, planes)
            picked[u, :, first : first + lanes] = part[u, t, :, :lanes].astype(jnp.bfloat16)
        take_right(slot, u)

    def solve(k, first_face, u=0):
        slot = order[k]
        solved = dot(picked[u], rhs[u])
        for c in range(parts):
            trace_r[k, c] = solved[:, c * LANE : (c + 1) * LANE]
        moved = dot(picked[u], padded[:, first_face * LANE :])
        for d in range(first_face, 3):
            turn_into(k, d, moved[:, (d - first_face) * LANE : (d - first_face + 1) * LANE], slot)

    def prepare_all(k):
        slot = order[k]
        take_right(slot)
        take_block(slot)
        solved = dot(inv[...], rhs[0])
        for c in range(parts):
            plain[k, c] = solved[:, c * LANE : (c + 1) * LANE]

            def put_plain(start, rows):
                trace_r[k, c, pl.ds(start, rows.shape[0]), :] = rows

            pick(plain.at[k, c], put_plain, 0, 1)
        spreads = dot(inv[...], padded[...])
        weight[k] = spreads.astype(jnp.bfloat16)
        for d in range(3):
            wide[d] = spreads[:, d * LANE : (d + 1) * LANE]

            def put_part(start, rows):
                part[0, d, pl.ds(start, rows.shape[0]), :] = rows

            pick(wide.at[d], put_part, 0, 1)
            turn_into(k, d, part[0, d], slot)

    def hop(k, c, axis):
        rows = pl.ds(axis * LANE, LANE)
        send, recv = ((x_send, x_recv), (y_send, y_recv))[axis]
        return pltpu.make_async_remote_copy(
            src_ref=out.at[k + 1, c, rows, :],
            dst_ref=inc.at[k, c, rows, :],
            send_sem=send.at[k, c],
            recv_sem=recv.at[k, c],
            device_id=((me_x + 1, me_y), (me_x, me_y + 1))[axis],
            device_id_type=MESH,
        )

    def advance(k, c):
        @pl.when(has_left)
        def _():
            hop(k, c, 0).wait_recv()

        @pl.when(has_below)
        def _():
            hop(k, c, 1).wait_recv()

        gone = dot(trace_m[k, :two, :two], inc[k, c])
        out[k + 1, c, :two, :] = (begun[c, :two, :] - gone).astype(jnp.bfloat16)
        send(k, c)

    def send(k, c):
        @pl.when(has_above)
        def _():
            hop(k, c, 1).start()

        @pl.when(has_right)
        def _():
            hop(k, c, 0).start()

    def follow(k):
        arrived = jnp.concatenate([inc[k, c] for c in range(parts)], axis=-1)
        gone = dot(trace_m[k, two:, :two], arrived)
        rising = [
            (begun[c, two:, :] - gone[:, c * LANE : (c + 1) * LANE]).astype(jnp.bfloat16) for c in range(parts)
        ]
        later = jnp.minimum(k + 1, planes - 1)
        lifted = dot(trace_m[later, :, two:], jnp.concatenate(rising, axis=-1))
        for c in range(parts):
            out[k + 1, c, two:, :] = rising[c]
            begun[c] = trace_r[later, c] - lifted[:, c * LANE : (c + 1) * LANE]

    def corner_sends(k):
        for c in range(parts):
            out[k + 1, c] = begun[c].astype(jnp.bfloat16)
        for c in range(parts):
            send(k, c)

    def corner_follow(k):
        rising = jnp.concatenate([begun[c, two:, :] for c in range(parts)], axis=-1).astype(jnp.bfloat16)
        later = jnp.minimum(k + 1, planes - 1)
        lifted = dot(trace_m[later, :, two:], rising)
        for c in range(parts):
            begun[c] = trace_r[later, c] - lifted[:, c * LANE : (c + 1) * LANE]

    def turn_faces(k, slot):
        faces = [[inc[k, c, d * LANE : (d + 1) * LANE, :] for c in range(parts)] for d in range(2)]
        faces.append([out[k, c, two:, :] for c in range(parts)])
        for d in range(3):
            face = jnp.concatenate(faces[d], axis=-1)
            turned[d * LANE : (d + 1) * LANE, :] = dot(table[orient[d, 0, slot]], face).astype(jnp.bfloat16)

    def finish_late(k):
        slot = order[k]
        take_block(slot)
        turn_faces(k, slot)
        lifted = dot(padded[...], turned[...])
        for t in range(parts):
            rows = stage[len(tiles) + t, pl.ds(slot, block, stride=planes), :]
            rhs[0, :, t * LANE : (t + 1) * LANE] = (rows - lifted[:, t * LANE : (t + 1) * LANE]).astype(jnp.bfloat16)
        swept = dot(inv[...], rhs[0])
        for c in range(parts):
            sol[c, pl.ds(k, block, stride=planes), :] = swept[:, c * LANE : (c + 1) * LANE]

    def finish(k):
        turn_faces(k, order[k])
        lifted = dot(weight[k], turned[...])
        for c in range(parts):
            sol[c, pl.ds(k, block, stride=planes), :] = plain[k, c] - lifted[:, c * LANE : (c + 1) * LANE]

    near = distance * 5 <= (count_x + count_y - 2) * 2
    neighbours = sum(p.astype(jnp.int32) for p in (has_left, has_right, has_below, has_above))

    def loop(start, stop, *works):
        def body(k, carry):
            for work in works:
                work(k)
            return carry

        lax.fori_loop(start, stop, body, 0)

    def advances(k):
        for c in range(parts):
            advance(k, c)

    def enter():
        pl.semaphore_wait(barrier, neighbours)
        begun[...] = trace_r[0]

    def prepare_pair(k):
        for u in range(2):
            gather(2 * k + u, u)
            solve(2 * k + u, 0, u)

    @pl.when(distance == 0)
    def _():
        last = planes - 1
        gather(0, 0)
        solve(0, 2, 0)
        enter()

        def two_steps(j):
            corner_sends(2 * j)

            @pl.when(j == 0)
            def _():
                gather(1, 1)

            solve(2 * j + 1, 2, 1)
            gather(jnp.minimum(2 * j + 2, last), 0)
            corner_follow(2 * j)
            corner_sends(2 * j + 1)
            solve(jnp.minimum(2 * j + 2, last), 2, 0)
            gather(jnp.minimum(2 * j + 3, last), 1)
            corner_follow(2 * j + 1)

        loop(0, planes // 2, two_steps)

    early = (distance > 0) & (distance * 10 <= (count_x + count_y - 2) * 3)

    @pl.when(early)
    def _():
        half = planes // 2
        loop(0, half // 2, prepare_pair)
        enter()

        def two_steps(j):
            advances(2 * j)

            @pl.when(j == 0)
            def _():
                gather(half)

            solve(half + j, 0)
            follow(2 * j)
            advances(2 * j + 1)
            follow(2 * j + 1)

            @pl.when(j < half - 1)
            def _():
                gather(half + 1 + j)

        loop(0, half, two_steps)

    @pl.when(near & (distance > 0) & jnp.logical_not(early))
    def _():
        loop(0, planes // 2, prepare_pair)
        enter()
        loop(0, planes, advances, follow)

    @pl.when(near)
    def _():
        loop(0, planes, finish_late)

    @pl.when(jnp.logical_not(near))
    def _():
        loop(0, planes, prepare_all)
        enter()
        loop(0, planes, advances, follow, finish)

    def drain(k, carry):
        for c in range(parts):
            @pl.when(has_right)
            def _():
                hop(k, c, 0).wait_send()

            @pl.when(has_above)
            def _():
                hop(k, c, 1).wait_send()
        return carry

    lax.fori_loop(0, planes, drain, 0)


def place_kernel(order, sol, out, ready, sems):
    block, planes, columns = ready.shape
    chunks = row_chunks(block)
    whole = block // LANE
    place_of = lax.broadcasted_iota(jnp.int32, (planes, LANE), 0)
    source = jnp.zeros((planes, LANE), jnp.int32)
    for k in range(planes):
        source = jnp.where(place_of == order[k], k, source)

    def put(i, start, size):
        rows = pl.ds(start, size)
        return pltpu.make_async_copy(ready.at[rows], out.at[rows], sems.at[i])

    def place(i, start, size):
        rows = pl.ds(start, size)
        picks = jnp.broadcast_to(source[None], (size, planes, LANE))
        for t in range(columns // LANE):
            lanes = slice(t * LANE, (t + 1) * LANE)
            swept = sol[t, pl.ds(start * planes, size * planes), :].reshape(size, planes, LANE)
            placed = jnp.take_along_axis(swept, picks, axis=1, mode="promise_in_bounds")
            ready[rows, :, lanes] = placed.astype(jnp.bfloat16)
        put(i, start, size).start()

    def place_full(i, carry):
        place(i, pl.multiple_of(i * LANE, LANE), LANE)
        return carry

    lax.fori_loop(0, whole, place_full, 0)
    for i, (start, size) in list(enumerate(chunks))[whole:]:
        place(i, start, size)
    for i, (start, size) in enumerate(chunks):
        put(i, start, size).wait()


def on_device(right_side, inverse_blocks, lift_matrix, plane_order, face_orient):
    rhs = jnp.transpose(right_side, (0, 1, 3, 2, 4))[0, 0]
    inv = jnp.transpose(inverse_blocks, (0, 1, 3, 2, 4))[0, 0]
    order = plane_order[0, 0]
    orient = jnp.transpose(face_orient, (0, 3, 1, 2))[0]
    block, planes, columns = rhs.shape
    tiles = pl.cdiv(block, LANE)
    chunks = len(row_chunks(block))
    parts = columns // LANE
    two, three = 2 * LANE, 3 * LANE
    bf16, f32 = jnp.bfloat16, jnp.float32
    table = jnp.asarray(orient_table(), bf16)
    lift = lift_matrix.T
    smem = pl.BlockSpec(memory_space=pltpu.SMEM)
    vmem = pl.BlockSpec(memory_space=pltpu.VMEM)
    anywhere = pl.BlockSpec(memory_space=pl.ANY)
    sol = pl.pallas_call(
        sweep_kernel,
        out_shape=pltpu.VMEM((parts, block * planes, LANE), f32),
        in_specs=[smem, smem] + [anywhere] * 4,
        out_specs=vmem,
        scratch_shapes=[
            pltpu.VMEM(table.shape, bf16),
            pltpu.VMEM(lift.shape, bf16),
            pltpu.VMEM(rhs.shape, bf16),
            pltpu.VMEM(inv.shape, bf16),
            pltpu.VMEM((tiles + parts, block * planes, LANE), f32),
            pltpu.VMEM((2, block, columns), bf16),
            pltpu.VMEM((block, block), bf16),
            pltpu.VMEM((block, three), bf16),
            pltpu.VMEM((three, columns), bf16),
            pltpu.VMEM((planes, parts, block, LANE), f32),
            pltpu.VMEM((3, block, LANE), f32),
            pltpu.VMEM((planes, block, three), bf16),
            pltpu.VMEM((2, max(tiles, 3), three, LANE), f32),
            pltpu.VMEM((2, three, block), bf16),
            pltpu.VMEM((planes, three, three), bf16),
            pltpu.VMEM((planes, parts, three, LANE), f32),
            pltpu.VMEM((parts, three, LANE), f32),
            pltpu.VMEM((planes, parts, two, LANE), bf16),
            pltpu.VMEM((planes + 1, parts, three, LANE), bf16),
            pltpu.SemaphoreType.DMA((2,)),
            pltpu.SemaphoreType.DMA((chunks,)),
            pltpu.SemaphoreType.DMA((chunks,)),
            pltpu.SemaphoreType.DMA((planes, parts)),
            pltpu.SemaphoreType.DMA((planes, parts)),
            pltpu.SemaphoreType.DMA((planes, parts)),
            pltpu.SemaphoreType.DMA((planes, parts)),
        ],
        compiler_params=pltpu.CompilerParams(
            collective_id=0, has_side_effects=True, vmem_limit_bytes=57 * 1024 * 1024
        ),
    )(order, orient, table, lift, rhs, inv)
    result = pl.pallas_call(
        place_kernel,
        out_shape=jax.ShapeDtypeStruct(rhs.shape, bf16),
        in_specs=[smem, vmem],
        out_specs=anywhere,
        scratch_shapes=[
            pltpu.VMEM(rhs.shape, bf16),
            pltpu.SemaphoreType.DMA((chunks,)),
        ],
        compiler_params=pltpu.CompilerParams(vmem_limit_bytes=16 * 1024 * 1024),
    )(order, sol)
    return jnp.transpose(result[None, None], (0, 1, 3, 2, 4))


def solution(mesh):
    placed = (
        P("gx", "gy", None, None, None),
        P("gx", "gy", None, None, None),
        P(),
        P("gx", "gy", None),
        P("gx", "gy", None, None),
    )
    return jax.shard_map(
        on_device,
        mesh=mesh,
        in_specs=placed,
        out_specs=P("gx", "gy", None, None, None),
        check_vma=False,
    )
```
